32 devices in a mesh: rows: 8 (over z, y), cols: 4 (over x, core).
Axes of the slice: x: 2, y: 2, z: 4, core: 2. Of those that a mesh axis runs over, the one named last changes fastest.
Arguments:
- factor: float32 [3328, 1664], P('rows', 'cols'), may hold values from -1 to 2, as said below
- slab: float32 [3328, 2048], P('rows', 'cols'), may hold values from -6 to 6
Outputs:
- result: float32 [3328, 2048], P('rows', 'cols')
The draws below stay inside these ranges and needn't reach their ends.
Inputs may be any that keep to these rules, and one draw needn't show every extreme that they name: factor is zero above the diagonal in its first 1664 rows; its diagonal entries lie between 1 and 2.
All inputs are finite; a program needn't handle non-finite values.
Results may differ from the reference program's by a relative error of at most 0.0001.
Values sent between devices are 32-bit elements; how exact they have to be, the bound alone decides.
No kernel may reach another device: no remote copies, remote signals or barrier semaphores. Data moves between devices by JAX's collectives and lax.ppermute only.
A program may use at most 64 MiB of HBM per device.

```python
import jax
import jax.numpy as jnp
from jax import lax

PB = 416
PANELS = 4
SLAB = 2048
K = 1664
N_ORDER = 3328


def draw_factor(key, part):
    key_off = jax.random.fold_in(key, 11)
    key_low = jax.random.fold_in(key, 12)
    key_diag = jax.random.fold_in(key, 13)
    shape = (N_ORDER, K)
    off_vals = jnp.clip(jax.random.normal(key_off, shape, jnp.float32), -4.0, 4.0) / jnp.sqrt(jnp.float32(K))
    low_vals = 0.6 * jnp.clip(jax.random.normal(key_low, shape, jnp.float32), -4.0, 4.0) / jnp.sqrt(jnp.float32(PB))
    diag_vals = jax.random.uniform(key_diag, shape, jnp.float32, 1.0, 2.0)
    row_ids = lax.broadcasted_iota(jnp.int32, shape, 0)
    col_ids = lax.broadcasted_iota(jnp.int32, shape, 1)
    row_block = row_ids // PB
    col_block = col_ids // PB
    row_in = row_ids % PB
    col_in = col_ids % PB
    inside = jnp.where(row_in > col_in, low_vals, jnp.where(row_in == col_in, diag_vals, 0.0))
    return jnp.where(row_block == col_block, inside, jnp.where(row_block > col_block, off_vals, 0.0)).astype(jnp.float32)


def shard_levels(key, dims, split, low, largest):
    factor_of = 1.0
    for axis_at, parts in split:
        steps = jax.random.uniform(jax.random.fold_in(jax.random.fold_in(key, 6), axis_at), (parts,), jnp.float32, low / len(split), largest / len(split))
        factor_of = factor_of * jnp.repeat(jnp.exp(steps), dims[axis_at] // parts).reshape((-1,) + (1,) * (len(dims) - 1 - axis_at))
    return factor_of


def normal_values(key, shape, spread, bound, split=(), held_as=jnp.bfloat16):
    loudness = shard_levels(key, shape, split, -0.22, 0.18) if split else 1.0
    values = jax.random.normal(key, shape, jnp.float32) * spread * loudness
    return jnp.minimum(jnp.maximum(values, -bound), bound).astype(held_as)


def setup_inputs(seed: int = 0) -> dict:
    arg_keys = jax.random.split(jax.random.key(seed), 3)
    return {
        "factor": draw_factor(jax.random.fold_in(arg_keys[2], 71), 0),
        "slab": normal_values(arg_keys[1], (N_ORDER, SLAB), 1.0, 6.0, ((0, 8), (1, 4)), jnp.float32),
    }


def reference(factor, slab):
    current = slab
    for panel in range(PANELS):
        offset = panel * PB
        panel_cols = factor[:, offset:offset + PB]
        solved = lax.linalg.triangular_solve(panel_cols[offset:offset + PB], current[offset:offset + PB], left_side=True, lower=True)
        current = current - jnp.dot(panel_cols, solved, precision=lax.Precision.HIGHEST)
        current = current.at[offset:offset + PB].set(solved)
    return current
```

```python
import functools

import jax
import jax.numpy as jnp
from jax import lax
from jax.experimental import pallas as pl
from jax.experimental.pallas import tpu as pltpu
from jax.sharding import PartitionSpec as P

PANELS = 4
CHUNKS = 2


def full_dot(a, b):
    return jnp.dot(a, b, precision=lax.Precision.HIGHEST, preferred_element_type=jnp.float32)


def dot(a, b):
    return jnp.dot(a, b, precision=lax.Precision.HIGH, preferred_element_type=jnp.float32)


def invert_kernel(base, lower_ref, out_ref):
    size = lower_ref.shape[0]
    count = size // base
    blocks = jnp.stack(
        [
            lower_ref[i * base : (i + 1) * base, i * base : (i + 1) * base]
            for i in range(count)
        ]
    )
    rows = lax.broadcasted_iota(jnp.int32, (count, base, base), 1)
    columns = lax.broadcasted_iota(jnp.int32, (count, base, base), 2)
    diagonal = jnp.sum(jnp.where(rows == columns, blocks, 0.0), axis=2, keepdims=True)
    scale = 1.0 / diagonal
    scaled = jnp.where(rows > columns, blocks, 0.0) * scale
    inverse = jnp.where(rows == columns, jnp.broadcast_to(scale, blocks.shape), 0.0)
    for step in range(base - 1):
        inverse = inverse - scaled[:, :, step : step + 1] * inverse[:, step : step + 1, :]
    out_ref[...] = jnp.zeros_like(out_ref)
    parts = []
    for i in range(count):
        out_ref[i * base : (i + 1) * base, i * base : (i + 1) * base] = inverse[i]
        parts.append((i * base, base))
    while len(parts) > 1:
        joined = []
        for i in range(0, len(parts) - 1, 2):
            (top, above), (middle, below) = parts[i], parts[i + 1]
            upper = slice(top, top + above)
            lower = slice(middle, middle + below)
            mixed = full_dot(lower_ref[lower, upper], out_ref[upper, upper])
            out_ref[lower, upper] = -full_dot(out_ref[lower, lower], mixed)
            joined.append((top, above + below))
        if len(parts) % 2:
            joined.append(parts[-1])
        parts = joined


def invert(block):
    base = next(b for b in (32, 16, 8, block.shape[0]) if block.shape[0] % b == 0)
    return pl.pallas_call(
        functools.partial(invert_kernel, base),
        out_shape=jax.ShapeDtypeStruct(block.shape, jnp.float32),
        in_specs=[pl.BlockSpec(memory_space=pltpu.VMEM)],
        out_specs=pl.BlockSpec(memory_space=pltpu.VMEM),
    )(block)


def body(levels, factor, slab):
    row = lax.axis_index("rows")
    column = lax.axis_index("cols")
    z, y = row // 2, row % 2
    x, k = column // 2, column % 2

    def send(value, target):
        pairs = []
        for sz in range(levels):
            for sy in range(2):
                for sx in range(2):
                    for sk in range(2):
                        to = target(sz, sy, sx, sk)
                        if to is not None:
                            tz, ty, tx, tk = to
                            pairs.append(
                                (
                                    ((sz * 2 + sy) * 2 + sx) * 2 + sk,
                                    ((tz * 2 + ty) * 2 + tx) * 2 + tk,
                                )
                            )
        return lax.ppermute(value, ("rows", "cols"), pairs)

    size = factor.shape[0]
    width = slab.shape[1] // CHUNKS
    chunks = range(CHUNKS)

    own = lax.cond((row == column) & (row < PANELS), invert, lambda v: v, factor)

    def across(sz, sy, sx, sk):
        if sz == 0:
            return (0, sy, 1, sk) if sx == 0 and (sy, sk) != (0, 1) else None
        return (sz, sy, 1 - sx, sk)

    def turn(sz, sy, sx, sk):
        return (sz, sk, sx, sy) if sz > 0 and sy != sk else None

    def cycle(sz, sy, sx, sk):
        if sy == sk:
            return (sz, 1 - sy, sx, sk)
        return (sz, sy, sx, 1 - sk)

    def cycle_or_swap(sz, sy, sx, sk):
        if sz == 0:
            return (0, sy, sx, 1 - sk)
        return cycle(sz, sy, sx, sk)

    from_x = send(own, across)
    turned = send(own, turn)
    cycled = send(own, lambda *d: cycle(*d) if d[0] > 0 else None)
    slab_turned = [send(slab[:, i * width : (i + 1) * width], turn) for i in chunks]
    near = jnp.where(x == 0, own, from_x)
    hopped = send(jnp.where(z == 0, near, from_x), cycle_or_swap)
    tb = jnp.where(y == k, own, turned)
    t2 = send(tb, lambda sz, sy, sx, sk: (sz, sy, 1 - sx, sk) if sz > 0 and sy != sk else None)
    t2 = jnp.where(y == k, from_x, t2)

    first = jnp.where(k == 0, near, hopped)
    second = jnp.where(k == 0, hopped, near)
    natural = [slab[:, i * width : (i + 1) * width] for i in chunks]
    inverse = jnp.where(y == 0, first, second)
    x0 = [dot(first, v) for v in natural]
    beside = [send(v, lambda sz, sy, sx, sk: (0, 1, sx, sk) if (sz, sy) == (0, 0) else None) for v in x0]
    x1 = [dot(second, v - dot(first, w)) for v, w in zip(natural, beside)]
    z0_result = [jnp.where(y == 0, a, b) for a, b in zip(x0, x1)]

    def pick(c):
        return jnp.where(
            x == c // 2,
            jnp.where(y == c % 2, tb, cycled),
            jnp.where(y == c % 2, t2, hopped),
        )

    blocks = [pick(c) for c in range(PANELS)]
    acc = [jnp.where(y == k, a, b) for a, b in zip(natural, slab_turned)]

    def to_partner(value, core, level):
        return send(
            value,
            lambda sz, sy, sx, sk: (sz, sy, sx, 1 - sk) if sz == level and sk == core else None,
        )

    def swap_below(value):
        return send(value, lambda sz, sy, sx, sk: (sz, sy, sx, 1 - sk) if sz > 1 else None)

    def down(value, core):
        if levels > 8:

            def one_level(_, carry):
                total, moving = carry
                moving = send(
                    moving,
                    lambda sz, sy, sx, sk: (sz + 1, sy, sx, sk)
                    if 0 < sz < levels - 1 and core in (None, sk)
                    else None,
                )
                return total + moving, moving

            return lax.fori_loop(0, levels - 2, one_level, (jnp.zeros_like(value), value))[0]
        total, moving = None, value
        for level in range(1, levels - 1):
            moving = send(
                moving,
                lambda sz, sy, sx, sk: (sz + 1, sy, sx, sk) if sz == level and core in (None, sk) else None,
            )
            total = moving if total is None else total + moving
        return total

    at_first = [
        send(v, lambda sz, sy, sx, sk: (1, sk, sx, 0) if (sz, sy) == (0, 0) else None) for v in x0
    ]
    at_second = [
        send(v, lambda sz, sy, sx, sk: (1, sk, sx, 1) if (sz, sy) == (0, 1) else None) for v in x1
    ]
    out = []
    for i in chunks:
        a0, a1 = at_first[i], at_second[i]
        d0 = down(a0, 0)
        d1 = down(a1, 1)
        pair = d0 + d1
        other = swap_below(pair)
        p0 = a0 + to_partner(a0, 0, 1) + jnp.where(k == 0, pair, other)
        p1 = a1 + to_partner(a1, 1, 1) + jnp.where(k == 0, other, pair)
        rest = acc[i] - dot(blocks[0], p0) - dot(blocks[1], p1)
        x2 = dot(blocks[2], rest)
        x2_here = to_partner(x2, 0, 1)
        x3 = dot(blocks[3], rest - dot(blocks[2], x2_here))
        solved = jnp.where(k == 0, x2, x3)
        q = down(solved, None)
        qo = swap_below(q)
        p2 = jnp.where(k == 0, q, qo)
        p3 = jnp.where(k == 0, qo, q)
        trailing = rest - dot(blocks[2], p2) - dot(blocks[3], p3)
        result = jnp.where(z == 1, solved, trailing)
        back = send(result, turn)
        result = jnp.where(y == k, result, back)
        out.append(jnp.where(z == 0, z0_result[i], result))
    return jnp.concatenate(out, axis=1)


def solution(mesh):
    return jax.shard_map(
        functools.partial(body, mesh.shape["rows"] // 2),
        mesh=mesh,
        in_specs=(P("rows", "cols"), P("rows", "cols")),
        out_specs=P("rows", "cols"),
        check_vma=False,
    )
```
